256 devices in a mesh: dp: 8 (over z), vocab: 32 (over y, x, core).
Axes of the slice: x: 4, y: 4, z: 8, core: 2. Of those that a mesh axis runs over, the one named last changes fastest.
Arguments:
- teacher_hidden: bfloat16 [1024, 16384], P('vocab', 'dp'), may hold values from -40 to 40
- teacher_weight: bfloat16 [16384, 65536], P('dp', 'vocab'), may hold values from -0.140625 to 0.140625
- student_hidden: bfloat16 [1024, 4096], P('vocab', 'dp'), may hold values from -40 to 40
- student_weight: bfloat16 [4096, 65536], P('dp', 'vocab'), may hold values from -0.28125 to 0.28125
Outputs:
- token_kl: float32 [1024], P('dp')
- weight_grad: bfloat16 [4096, 65536], P('dp', 'vocab')
The draws below stay inside these ranges and needn't reach their ends.
All inputs are finite; a program needn't handle non-finite values.
Results may differ from the reference program's by a relative error of at most 0.005.
Values may be sent and summed in bfloat16 or wider, within the bound.
A program may use at most 128 MiB of HBM per device.

```python
import math
import jax
import jax.numpy as jnp

D = 4096
DT = 16384
V = 65536
TOKENS = 1024
GRAD_SCALE = 16384


def column_of(weight_key, column, height):
    values = jax.random.normal(jax.random.fold_in(weight_key, column), (height,), jnp.float32)
    values = jnp.clip(values, -6.0, 6.0)
    places = jnp.arange(height)
    values = jnp.where((column == 0) & (places == 0), 6.0, values)
    values = jnp.where((column == 0) & (places == 1), -6.0, values)
    return values * (3.0 / math.sqrt(height))


def whole_weight(key, stream, height):
    weight_key = jax.random.fold_in(key, stream)
    columns = jax.vmap(lambda column: column_of(weight_key, column, height))(jnp.arange(V))
    return columns.T.astype(jnp.bfloat16)


def draw_teacher_weight(key, part):
    return whole_weight(key, 101, DT)


def draw_student_weight(key, part):
    return whole_weight(key, 202, D)


def draw_teacher_hidden(key, part):
    drawn = jax.random.normal(jax.random.fold_in(key, 1), (TOKENS, DT), jnp.float32)
    return jnp.clip(drawn, -6.0, 6.0).astype(jnp.bfloat16)


def draw_student_hidden(key, part):
    drawn = jax.random.normal(jax.random.fold_in(key, 2), (TOKENS, D), jnp.float32)
    return jnp.clip(drawn, -6.0, 6.0).astype(jnp.bfloat16)


def setup_inputs(seed: int = 0) -> dict:
    arg_keys = jax.random.split(jax.random.key(seed), 5)
    teacher_hidden = draw_teacher_hidden(jax.random.fold_in(arg_keys[4], 71), 0)
    teacher_weight = draw_teacher_weight(jax.random.fold_in(arg_keys[4], 71), 0)
    student_hidden = draw_student_hidden(jax.random.fold_in(arg_keys[4], 71), 0)
    student_weight = draw_student_weight(jax.random.fold_in(arg_keys[4], 71), 0)
    return {"teacher_hidden": teacher_hidden, "teacher_weight": teacher_weight, "student_hidden": student_hidden, "student_weight": student_weight}


def reference(teacher_hidden, teacher_weight, student_hidden, student_weight):
    teacher_logits = jnp.dot(teacher_hidden, teacher_weight, preferred_element_type=jnp.float32)
    student_logits = jnp.dot(student_hidden, student_weight, preferred_element_type=jnp.float32)
    teacher_top = jnp.max(teacher_logits, axis=1)
    student_top = jnp.max(student_logits, axis=1)
    teacher_exp = jnp.exp(teacher_logits - teacher_top[:, None])
    teacher_total = jnp.sum(teacher_exp, axis=1)
    numerator = jnp.sum(teacher_exp * (teacher_logits - student_logits), axis=1)
    student_total = jnp.sum(jnp.exp(student_logits - student_top[:, None]), axis=1)
    teacher_lse = teacher_top + jnp.log(teacher_total)
    student_lse = student_top + jnp.log(student_total)
    token_kl = numerator / teacher_total - teacher_lse + student_lse
    factor = GRAD_SCALE / TOKENS
    teacher_prob = jnp.exp(teacher_logits - teacher_lse[:, None])
    student_prob = jnp.exp(student_logits - student_lse[:, None])
    deltas = (factor * (student_prob - teacher_prob)).astype(jnp.bfloat16)
    weight_grad = jnp.dot(student_hidden.T, deltas, preferred_element_type=jnp.float32)
    return token_kl, weight_grad.astype(jnp.bfloat16)
```

```python
import functools

import jax
import jax.numpy as jnp
from jax import lax
from jax.experimental import pallas as pl
from jax.experimental.pallas import tpu as pltpu
from jax.sharding import PartitionSpec as P

BF16 = jnp.bfloat16
F32 = jnp.float32
SCALE = 2.0**-7.75
LOG2E = 1.4426950408889634


def encode(x):
    t = jnp.abs(x) * SCALE + SCALE
    t = t * t
    t = t * t
    t = t * t
    t = t * t
    return jnp.where(x < 0, -t, t).astype(BF16)


def decode(word):
    y = word.astype(F32)
    t = jnp.exp2(jnp.log(jnp.abs(y)) * (LOG2E / 16) + 7.75) - 1.0
    return jnp.where(y < 0, -t, t)


def kernel(
    dims,
    th_hbm, tw_hbm, sh_hbm, sw_hbm,
    kl_out, grad_out,
    th, tw, sh, sw, pst, ptt, r_s, r_t, s_s, s_t, dl, acc, sht, stats,
    local_sem, hid_send, hid_recv, rel_send, rel_recv,
    s_send, s_recv, t_send, t_recv, st_send, st_recv, ag_send, ag_recv,
):
    nz, nv, cpq, gr, ks, kt, cq, tc, factor = dims
    nch = nv // 2
    n_items = 4 * (nz // 2 - 1) + 2
    p = lax.axis_index("dp")
    v = lax.axis_index("vocab")
    core = lax.rem(v, 2)
    chip = v // 2
    partner = v + 1 - 2 * core
    right, left = lax.rem(p + 1, nz), lax.rem(p + nz - 1, nz)
    ways = ((1, right), (-1, left))

    def at(offset):
        return lax.rem(p + offset + 2 * nz, nz)

    load_sw = pltpu.make_async_copy(sw_hbm, sw, local_sem.at[0])
    load_sh = pltpu.make_async_copy(sh_hbm, sh.at[core, chip], local_sem.at[1])
    load_th = pltpu.make_async_copy(th_hbm, th.at[core, chip], local_sem.at[2])
    load_sh.start()
    load_th.start()
    load_sw.start()
    n_tw = tw.shape[0]
    load_tw = [
        pltpu.make_async_copy(tw_hbm.at[:, j * tc : (j + 1) * tc], tw.at[j], local_sem.at[3 + j])
        for j in range(n_tw)
    ]
    for load in load_tw:
        load.start()

    barrier = pltpu.get_barrier_semaphore()

    def greet(j, _):
        pl.semaphore_signal(barrier, inc=1, device_id={"vocab": lax.rem(v + j, nv)})
        return 0

    lax.fori_loop(1, nv, greet, 0)
    for _, neighbour in ways:
        pl.semaphore_signal(barrier, inc=1, device_id={"dp": neighbour})
    pl.semaphore_wait(barrier, nv + 1)

    def spread(source, target, k):
        def one(j, _):
            peer = lax.rem(chip + j, nch)
            pltpu.make_async_remote_copy(
                source, target.at[core, chip], hid_send.at[k], hid_recv.at[k],
                device_id={"vocab": 2 * peer + core},
            ).start()
            return 0

        lax.fori_loop(1, nch, one, 0)

    def others(target, k):
        block = target.at[core, pl.ds(0, nch - 1)]
        return pltpu.make_async_remote_copy(
            block, block, hid_send.at[k], hid_recv.at[k], device_id={"vocab": partner}
        )

    def relay(target, k, slab):
        return pltpu.make_async_remote_copy(
            target.at[slab], target.at[slab], rel_send.at[k], rel_recv.at[k],
            device_id={"vocab": partner},
        )

    spread(sh_hbm, sh, 0)
    spread(th_hbm, th, 1)
    load_sh.wait()
    others(sh, 0).wait_recv()
    relay(sh, 0, core).start()
    load_sw.wait()
    relay(sh, 0, 1 - core).wait_recv()

    def student_block(q):
        rows = sh[:, pl.ds(cpq * q, cpq)].reshape(2 * gr, ks)
        for n in range(4):
            part = jnp.dot(rows, sw[:, n * cq : (n + 1) * cq], preferred_element_type=F32)
            pst[q, :, n] = part.reshape(2, gr, cq)

    def teacher_part(g, j):
        rows = th[g].reshape(nz * gr, kt)
        part = jnp.dot(rows, tw[j], preferred_element_type=F32)
        per = cq // tc
        cols = pl.ds(pl.multiple_of(lax.rem(j, per) * tc, tc), tc)
        ptt[:, g, j // per, :, cols] = part.reshape(nz, gr, tc)

    def student_copy(d, i, neighbour):
        return pltpu.make_async_remote_copy(
            s_s.at[d, i], r_s.at[d, i], s_send, s_recv.at[d, i], device_id={"dp": neighbour}
        )

    def teacher_copy(g, d, i, neighbour):
        return pltpu.make_async_remote_copy(
            s_t.at[g, d, i], r_t.at[g, d, i], t_send.at[g], t_recv.at[g, d, i],
            device_id={"dp": neighbour},
        )

    def student_items(lo, hi, more=None):
        def one(i, _):
            k = nz // 2 - (i + 2) // 4
            for d, (sign, neighbour) in enumerate(ways):
                n = lax.rem(i + 2 * d, 4)
                x = pst[at(sign * k), :, n]
                if lo >= 4:
                    student_copy(d, i - 4, neighbour).wait_recv()
                    x = x + decode(r_s[d, i - 4])
                s_s[d, i] = encode(x)
                student_copy(d, i, neighbour).start()
            if more is not None:
                more(i)
            return 0

        lax.fori_loop(lo, hi, one, 0)

    def student_end():
        def one(j, _):
            i = n_items - 4 + j
            for d, (_, neighbour) in enumerate(ways):
                n = lax.rem(i + 2 * d, 4)
                student_copy(d, i, neighbour).wait_recv()
                pst[p, :, n] = pst[p, :, n] + decode(r_s[d, i])
            return 0

        lax.fori_loop(0, 4, one, 0)

    def teacher_items(g, lo, hi, more=None):
        def one(i, _):
            k = nz // 2 - (i + 2) // 4
            for d, (sign, neighbour) in enumerate(ways):
                n = lax.rem(i + 2 * d, 4)
                x = ptt[at(sign * k), g, n]
                if lo >= 4:
                    teacher_copy(g, d, i - 4, neighbour).wait_recv()
                    x = x + decode(r_t[g, d, i - 4])
                s_t[g, d, i] = encode(x)
                teacher_copy(g, d, i, neighbour).start()
            if more is not None:
                more(i)
            return 0

        lax.fori_loop(lo, hi, one, 0)

    def teacher_end(g):
        def one(j, _):
            i = n_items - 4 + j
            for d, (_, neighbour) in enumerate(ways):
                n = lax.rem(i + 2 * d, 4)
                teacher_copy(g, d, i, neighbour).wait_recv()
                ptt[p, g, n] = ptt[p, g, n] + decode(r_t[g, d, i])
            return 0

        lax.fori_loop(0, 4, one, 0)

    def stats_start(g):
        t_top = jnp.full((gr, 1), -jnp.inf, F32)
        s_top = t_top
        for n in range(4):
            t_top = jnp.maximum(t_top, jnp.max(ptt[p, g, n], axis=1, keepdims=True))
            s_top = jnp.maximum(s_top, jnp.max(pst[p, g, n], axis=1, keepdims=True))
        t_sum = jnp.zeros((gr, 1), F32)
        t_num, s_sum = t_sum, t_sum
        for n in range(4):
            t, s = ptt[p, g, n], pst[p, g, n]
            e = jnp.exp(t - t_top)
            t_sum = t_sum + jnp.sum(e, axis=1, keepdims=True)
            t_num = t_num + jnp.sum(e * (t - s), axis=1, keepdims=True)
            s_sum = s_sum + jnp.sum(jnp.exp(s - s_top), axis=1, keepdims=True)
        lane = lax.broadcasted_iota(jnp.int32, (gr, 128), 1)
        table = jnp.zeros((gr, 128), F32)
        for place, column in ((0, t_top), (1, t_top), (2, s_top), (8, t_sum), (9, t_num), (10, s_sum)):
            table = jnp.where(lane == place, column, table)
        stats[g, v] = jnp.concatenate([table] * (128 // gr), axis=0).T[:16]

        def one(j, _):
            pltpu.make_async_remote_copy(
                stats.at[g, v], stats.at[g, v], st_send.at[g], st_recv.at[g],
                device_id={"vocab": lax.rem(v + j, nv)},
            ).start()
            return 0

        lax.fori_loop(1, nv, one, 0)

    def stats_copy(g):
        block = stats.at[g, pl.ds(0, nv - 1)]
        return pltpu.make_async_remote_copy(
            block, block, st_send.at[g], st_recv.at[g], device_id={"vocab": partner}
        )

    def deltas(g):
        stats_copy(g).wait_recv()
        tops = stats[g, :, 0:8]
        top = jnp.max(tops, axis=0)
        total = jnp.sum(jnp.exp(tops - top[None]) * stats[g, :, 8:16], axis=0)
        lse = top + jnp.log(total)
        kl_out[g : g + 1, :] = total[1:2] / total[0:1] - lse[0:1] + lse[2:3]
        turned = jnp.concatenate([lse] * 16, axis=0).T
        t_lse, s_lse = turned[:gr, 0:1], turned[:gr, 2:3]
        for n in range(4):
            student = jnp.exp(pst[p, g, n] - s_lse)
            teacher = jnp.exp(ptt[p, g, n] - t_lse)
            dl[g, n, p] = (factor * (student - teacher)).astype(BF16)

    def delta_copy(g, d, i, sign, neighbour):
        n = lax.rem(i + 2 * d, 4)
        block = dl.at[g, n, at(-sign * (i // 4))]
        return pltpu.make_async_remote_copy(
            block, block, ag_send.at[g], ag_recv.at[g, d, i], device_id={"dp": neighbour}
        )

    def arrived(g, d, i, sign, neighbour):
        n = lax.rem(i + 2 * d, 4)
        block = dl.at[g, n, at(-sign * (i // 4 + 1))]
        return pltpu.make_async_remote_copy(
            block, block, ag_send.at[g], ag_recv.at[g, d, i], device_id={"dp": neighbour}
        )

    def delta_items(g, lo, hi):
        def one(i, _):
            for d, (sign, neighbour) in enumerate(ways):
                if lo >= 4:
                    arrived(g, d, i - 4, sign, neighbour).wait_recv()
                delta_copy(g, d, i, sign, neighbour).start()
            return 0

        lax.fori_loop(lo, hi, one, 0)

    def delta_end(g):
        def one(i, _):
            for d, (sign, neighbour) in enumerate(ways):
                arrived(g, d, i, sign, neighbour).wait_recv()
            return 0

        lax.fori_loop(n_items - 4, n_items, one, 0)

    def grad_part(g, n):
        part = jnp.dot(sht[g], dl[g, n].reshape(nz * gr, cq), preferred_element_type=F32)
        if g == 0:
            acc[n] = part
        else:
            grad_out[:, n * cq : (n + 1) * cq] = (acc[n] + part).astype(BF16)

    last = n_items
    mid = max(4, last - 4)
    student_block(at(nz // 2))
    student_items(0, 2)
    for k in range(nz // 2 - 1, 0, -1):
        student_block(at(k))
        student_block(at(-k))
        if k == nz // 2 - 1:
            student_items(2, 4)
    student_block(p)
    for g in range(2):
        sht[g] = sh[g].reshape(nz * gr, ks).T
    student_items(4, mid)
    load_th.wait()
    others(th, 1).wait_recv()
    relay(th, 1, core).start()
    student_items(mid, last)
    for load in load_tw:
        load.wait()
    relay(th, 1, 1 - core).wait_recv()

    def teacher_first(j, _):
        teacher_part(0, j)
        return 0

    lax.fori_loop(0, n_tw, teacher_first, 0)
    teacher_items(0, 0, 4)
    student_end()

    def teacher_second(j, _):
        teacher_part(1, j)
        return 0

    lax.fori_loop(0, n_tw // 4, teacher_second, 0)
    teacher_items(0, 4, last)
    lax.fori_loop(n_tw // 4, n_tw, teacher_second, 0)
    teacher_items(1, 0, 4)
    teacher_end(0)
    stats_start(0)
    teacher_items(1, 4, mid)
    deltas(0)
    delta_items(0, 0, 4)
    teacher_items(1, mid, last)
    teacher_end(1)
    stats_start(1)
    delta_items(0, 4, mid)
    deltas(1)
    delta_items(1, 0, 4)
    delta_items(0, mid, last)
    delta_end(0)
    for n in range(4):
        grad_part(0, n)
    delta_items(1, 4, last)
    delta_end(1)
    for n in range(4):
        grad_part(1, n)

    others(sh, 0).wait_send()
    others(th, 1).wait_send()
    relay(sh, 0, core).wait_send()
    relay(th, 1, core).wait_send()
    pltpu.make_async_remote_copy(
        s_s, r_s, s_send, s_recv.at[0, 0], device_id={"dp": right}
    ).wait_send()
    for g in range(2):
        stats_copy(g).wait_send()
        for sem in (t_send, ag_send):
            pltpu.make_async_remote_copy(
                s_t.at[g], r_t.at[g], sem.at[g], t_recv.at[g, 0, 0], device_id={"dp": right}
            ).wait_send()


def body(teacher_hidden, teacher_weight, student_hidden, student_weight):
    nz, nv = lax.axis_size("dp"), lax.axis_size("vocab")
    rows, kt = teacher_hidden.shape
    ks, width = student_weight.shape
    nch = nv // 2
    cpq = nch // nz
    gr = cpq * rows
    cq = width // 4
    tc = min(256, cq)
    n_items = 4 * (nz // 2 - 1) + 2
    factor = float(width * nv // 4 / (rows * nv))
    dims = (nz, nv, cpq, gr, ks, kt, cq, tc, factor)
    dma = pltpu.SemaphoreType.DMA
    any_space = pl.BlockSpec(memory_space=pl.ANY)
    vmem = pl.BlockSpec(memory_space=pltpu.VMEM)
    kl, grad = pl.pallas_call(
        functools.partial(kernel, dims),
        out_shape=(
            jax.ShapeDtypeStruct((2, 128), F32),
            jax.ShapeDtypeStruct((ks, width), BF16),
        ),
        in_specs=[any_space] * 4,
        out_specs=(vmem, vmem),
        scratch_shapes=[
            pltpu.VMEM((2, nch, rows, kt), BF16),
            pltpu.VMEM((width // tc, kt, tc), BF16),
            pltpu.VMEM((2, nch, rows, ks), BF16),
            pltpu.VMEM((ks, width), BF16),
            pltpu.VMEM((nz, 2, 4, gr, cq), F32),
            pltpu.VMEM((nz, 2, 4, gr, cq), F32),
            pltpu.VMEM((2, n_items, 2, gr, cq), BF16),
            pltpu.VMEM((2, 2, n_items, gr, cq), BF16),
            pltpu.VMEM((2, n_items, 2, gr, cq), BF16),
            pltpu.VMEM((2, 2, n_items, gr, cq), BF16),
            pltpu.VMEM((2, 4, nz, gr, cq), BF16),
            pltpu.VMEM((4, ks, cq), F32),
            pltpu.VMEM((2, ks, nz * gr), BF16),
            pltpu.VMEM((2, nv, 16, 128), F32),
            dma((3 + width // tc,)),
            dma((2,)),
            dma((2,)),
            dma((2,)),
            dma((2,)),
            dma,
            dma((2, n_items)),
            dma((2,)),
            dma((2, 2, n_items)),
            dma((2,)),
            dma((2,)),
            dma((2,)),
            dma((2, 2, n_items)),
        ],
        compiler_params=pltpu.CompilerParams(
            collective_id=0, has_side_effects=True, vmem_limit_bytes=67_000_000
        ),
        name="distill",
    )(teacher_hidden, teacher_weight, student_hidden, student_weight)
    token_kl = kl[:, :gr].reshape(2, cpq, rows).transpose(1, 0, 2).reshape(2 * gr)
    return token_kl, grad


def solution(mesh):
    placed = (P("vocab", "dp"), P("dp", "vocab"), P("vocab", "dp"), P("dp", "vocab"))
    return jax.shard_map(
        body, mesh=mesh, in_specs=placed, out_specs=(P("dp"), P("dp", "vocab")), check_vma=False
    )
```

```python
import functools

import jax
import jax.numpy as jnp
from jax import lax
from jax.experimental import pallas as pl
from jax.experimental.pallas import tpu as pltpu
from jax.sharding import PartitionSpec as P

BF16 = jnp.bfloat16
F32 = jnp.float32
SCALE = 2.0**-7.75
LOG2E = 1.4426950408889634


def encode(x):
    t = jnp.abs(x) * SCALE + SCALE
    t = t * t
    t = t * t
    t = t * t
    t = t * t
    return jnp.where(x < 0, -t, t).astype(BF16)


def decode(word):
    y = word.astype(F32)
    t = jnp.exp2(jnp.log(jnp.abs(y)) * (LOG2E / 16) + 7.75) - 1.0
    return jnp.where(y < 0, -t, t)


def kernel(
    dims,
    th_hbm, tw_hbm, sh_hbm, sw_hbm,
    kl_out, grad_out,
    th, tw, sh, sw, pst, ptt, r_s, r_t, s_s, s_t, dl, acc, sht, stats, stage,
    local_sem, hid_send, hid_recv, rel_send, rel_recv, out_sem,
    s_send, s_recv, t_send, t_recv, st_send, st_recv, ag_send, ag_recv,
):
    nz, nv, cpq, gr, ks, kt, cq, tc, factor = dims
    nch = nv // 2
    n_items = 4 * (nz // 2 - 1) + 2
    p = lax.axis_index("dp")
    v = lax.axis_index("vocab")
    core = lax.rem(v, 2)
    chip = v // 2
    partner = v + 1 - 2 * core
    right, left = lax.rem(p + 1, nz), lax.rem(p + nz - 1, nz)
    ways = ((1, right), (-1, left))

    def at(offset):
        return lax.rem(p + offset + 2 * nz, nz)

    load_sw = pltpu.make_async_copy(sw_hbm, sw, local_sem.at[0])
    load_sh = pltpu.make_async_copy(sh_hbm, sh.at[core, chip], local_sem.at[1])
    load_th = pltpu.make_async_copy(th_hbm, th.at[core, chip], local_sem.at[2])
    load_sh.start()
    load_th.start()
    load_sw.start()
    n_tw = tw.shape[0]
    load_tw = [
        pltpu.make_async_copy(tw_hbm.at[:, j * tc : (j + 1) * tc], tw.at[j], local_sem.at[3 + j])
        for j in range(n_tw)
    ]
    for load in load_tw:
        load.start()

    barrier = pltpu.get_barrier_semaphore()

    def greet(j, _):
        pl.semaphore_signal(barrier, inc=1, device_id={"vocab": lax.rem(v + j, nv)})
        return 0

    lax.fori_loop(1, nv, greet, 0)
    for _, neighbour in ways:
        pl.semaphore_signal(barrier, inc=1, device_id={"dp": neighbour})
    pl.semaphore_wait(barrier, nv + 1)

    def spread(source, target, k, arrival):
        def one(j, _):
            peer = lax.rem(chip + j, nch)
            pltpu.make_async_remote_copy(
                source, target.at[core, chip], hid_send.at[k], arrival,
                device_id={"vocab": 2 * peer + core},
            ).start()
            return 0

        lax.fori_loop(1, nch, one, 0)

    def others(target, k, arrival):
        block = target.at[core, pl.ds(0, nch - 1)]
        return pltpu.make_async_remote_copy(
            block, block, hid_send.at[k], arrival, device_id={"vocab": partner}
        )

    def relay(target, k, slab):
        return pltpu.make_async_remote_copy(
            target.at[slab], target.at[slab], rel_send.at[k], rel_recv.at[k],
            device_id={"vocab": partner},
        )

    spread(sh_hbm, sh, 0, hid_recv.at[chip])
    spread(th_hbm, th, 1, hid_recv.at[nch])
    load_sh.wait()
    load_sw.wait()

    def student_block(q):
        for j in range(cpq):
            source = cpq * q + j

            @pl.when(source != chip)
            def _():
                block = sh.at[core, source]
                pltpu.make_async_remote_copy(
                    block, block, hid_send.at[0], hid_recv.at[source], device_id={"vocab": partner}
                ).wait_recv()

        rows = sh[core, pl.ds(cpq * q, cpq)].reshape(gr, ks)
        for n in range(4):
            part = jnp.dot(rows, sw[:, n * cq : (n + 1) * cq], preferred_element_type=F32)
            pst[q, core, n] = part

    def student_rest():
        rows = sh[1 - core].reshape(nz * gr, ks)
        for n in range(4):
            part = jnp.dot(rows, sw[:, n * cq : (n + 1) * cq], preferred_element_type=F32)
            pst[:, 1 - core, n] = part.reshape(nz, gr, cq)

    def teacher_part(g, j):
        rows = th[g].reshape(nz * gr, kt)
        part = jnp.dot(rows, tw[j], preferred_element_type=F32)
        per = cq // tc
        cols = pl.ds(pl.multiple_of(lax.rem(j, per) * tc, tc), tc)
        ptt[:, g, j // per, :, cols] = part.reshape(nz, gr, tc)

    student = (pst, s_s, r_s, s_send, s_recv)
    teacher = (ptt, s_t, r_t, t_send, t_recv)

    def ring_copy(which, g, d, i, neighbour):
        _, out, landed, sent, got = which
        return pltpu.make_async_remote_copy(
            out.at[g, d, i], landed.at[g, d, i], sent.at[g], got.at[g, d, i],
            device_id={"dp": neighbour},
        )

    def ring_items(which, g, lo, hi, more=None):
        part, out, landed, _, _ = which

        def one(i, _):
            k = nz // 2 - (i + 2) // 4
            for d, (sign, neighbour) in enumerate(ways):
                n = lax.rem(i + 2 * d, 4)
                x = part[at(sign * k), g, n]
                if lo >= 4:
                    ring_copy(which, g, d, i - 4, neighbour).wait_recv()
                    x = x + decode(landed[g, d, i - 4])
                out[g, d, i] = encode(x)
                ring_copy(which, g, d, i, neighbour).start()
            if more is not None:
                more(i)
            return 0

        lax.fori_loop(lo, hi, one, 0)

    def ring_end(which, g):
        part, _, landed, _, _ = which

        def one(j, _):
            i = n_items - 4 + j
            for d, (_, neighbour) in enumerate(ways):
                n = lax.rem(i + 2 * d, 4)
                ring_copy(which, g, d, i, neighbour).wait_recv()
                part[p, g, n] = part[p, g, n] + decode(landed[g, d, i])
            return 0

        lax.fori_loop(0, 4, one, 0)

    def stats_start(g):
        t_top = jnp.full((gr, 1), -jnp.inf, F32)
        s_top = t_top
        for n in range(4):
            t_top = jnp.maximum(t_top, jnp.max(ptt[p, g, n], axis=1, keepdims=True))
            s_top = jnp.maximum(s_top, jnp.max(pst[p, g, n], axis=1, keepdims=True))
        t_sum = jnp.zeros((gr, 1), F32)
        t_num, s_sum = t_sum, t_sum
        for n in range(4):
            t, s = ptt[p, g, n], pst[p, g, n]
            e = jnp.exp(t - t_top)
            t_sum = t_sum + jnp.sum(e, axis=1, keepdims=True)
            t_num = t_num + jnp.sum(e * (t - s), axis=1, keepdims=True)
            s_sum = s_sum + jnp.sum(jnp.exp(s - s_top), axis=1, keepdims=True)
        lane = lax.broadcasted_iota(jnp.int32, (gr, 128), 1)
        table = jnp.zeros((gr, 128), F32)
        for place, column in ((0, t_top), (1, t_top), (2, s_top), (8, t_sum), (9, t_num), (10, s_sum)):
            table = jnp.where(lane == place, column, table)
        sides = [table[r : r + gr // cpq] for r in range(0, gr, gr // cpq) for _ in range(2)]
        stats[g, v] = jnp.concatenate(sides * (64 // gr), axis=0).T[:16]

        def one(j, _):
            pltpu.make_async_remote_copy(
                stats.at[g, v], stats.at[g, v], st_send.at[g], st_recv.at[g],
                device_id={"vocab": lax.rem(v + j, nv)},
            ).start()
            return 0

        lax.fori_loop(1, nv, one, 0)

    def stats_copy(g):
        block = stats.at[g, pl.ds(0, nv - 1)]
        return pltpu.make_async_remote_copy(
            block, block, st_send.at[g], st_recv.at[g], device_id={"vocab": partner}
        )

    def deltas(g):
        stats_copy(g).wait_recv()
        tops = stats[g, :, 0:8]
        top = jnp.max(tops, axis=0)
        total = jnp.sum(jnp.exp(tops - top[None]) * stats[g, :, 8:16], axis=0)
        lse = top + jnp.log(total)
        kl = total[1:2] / total[0:1] - lse[0:1] + lse[2:3]
        if g == 0:
            kl_out[...] = kl
        else:
            lane = lax.broadcasted_iota(jnp.int32, (1, 128), 1)
            kl_out[...] = jnp.where(lane // (gr // cpq) % 2 == 1, kl, kl_out[...])
        turned = jnp.concatenate([lse] * 16, axis=0).T
        rows = gr // cpq
        turned = jnp.concatenate([turned[2 * r : 2 * r + rows] for r in range(0, gr, rows)], axis=0)
        t_lse, s_lse = turned[:, 0:1], turned[:, 2:3]
        for n in range(4):
            by_student = jnp.exp(pst[p, g, n] - s_lse)
            by_teacher = jnp.exp(ptt[p, g, n] - t_lse)
            dl[g, n, p] = (factor * (by_student - by_teacher)).astype(BF16)

    def delta_copy(g, d, i, sign, neighbour):
        n = lax.rem(i + 2 * d, 4)
        block = dl.at[g, n, at(-sign * (i // 4))]
        return pltpu.make_async_remote_copy(
            block, block, ag_send.at[g], ag_recv.at[g, d, i], device_id={"dp": neighbour}
        )

    def arrived(g, d, i, sign, neighbour):
        n = lax.rem(i + 2 * d, 4)
        block = dl.at[g, n, at(-sign * (i // 4 + 1))]
        return pltpu.make_async_remote_copy(
            block, block, ag_send.at[g], ag_recv.at[g, d, i], device_id={"dp": neighbour}
        )

    def delta_items(g, lo, hi):
        def one(i, _):
            for d, (sign, neighbour) in enumerate(ways):
                if lo >= 4:
                    arrived(g, d, i - 4, sign, neighbour).wait_recv()
                delta_copy(g, d, i, sign, neighbour).start()
            return 0

        lax.fori_loop(lo, hi, one, 0)

    def delta_end(g, lo, hi):
        def one(i, _):
            for d, (sign, neighbour) in enumerate(ways):
                arrived(g, d, i, sign, neighbour).wait_recv()
            return 0

        lax.fori_loop(lo, hi, one, 0)

    def grad_copy(n):
        return pltpu.make_async_copy(
            stage.at[n], grad_out.at[:, n * cq : (n + 1) * cq], out_sem.at[n]
        )

    def grad_part(g, n):
        part = jnp.dot(sht[g], dl[g, n].reshape(nz * gr, cq), preferred_element_type=F32)
        if g == 0:
            acc[n] = part
        else:
            stage[n] = (acc[n] + part).astype(BF16)
            grad_copy(n).start()

    last = n_items
    mid = max(4, last - 4)
    other = 1 - core
    student_block(at(nz // 2))
    ring_items(student, core, 0, 2)
    for k in range(nz // 2 - 1, 0, -1):
        student_block(at(k))
        student_block(at(-k))
        if k == nz // 2 - 1:
            ring_items(student, core, 2, 4)
    student_block(p)
    relay(sh, 0, core).start()
    ring_items(student, core, 4, mid)
    relay(sh, 0, other).wait_recv()
    student_rest()
    ring_items(student, other, 0, 4)
    ring_items(student, core, mid, last)
    load_th.wait()
    others(th, 1, hid_recv.at[nch]).wait_recv()
    relay(th, 1, core).start()
    ring_end(student, core)
    for load in load_tw:
        load.wait()

    def teacher_own(i):
        @pl.when(i - 4 < n_tw)
        def _():
            teacher_part(core, i - 4)

    def teacher_rest(j, _):
        teacher_part(other, j)
        return 0

    ring_items(student, other, 4, last, teacher_own)
    for j in range(last - 4, n_tw):
        teacher_part(core, j)
    for g in range(2):
        sht[g] = sh[g].reshape(nz * gr, ks).T
    relay(th, 1, other).wait_recv()
    lax.fori_loop(0, n_tw, teacher_rest, 0)
    ring_items(teacher, 0, 0, 4)
    ring_end(student, other)
    ring_items(teacher, 0, 4, last)
    ring_items(teacher, 1, 0, 4)
    ring_end(teacher, 0)
    stats_start(0)
    ring_items(teacher, 1, 4, mid)
    deltas(0)
    delta_items(0, 0, 4)
    ring_items(teacher, 1, mid, last)
    ring_end(teacher, 1)
    stats_start(1)
    delta_items(0, 4, mid)
    deltas(1)
    delta_items(1, 0, 4)
    delta_items(0, mid, last)
    delta_items(1, 4, mid)
    delta_end(0, last - 4, last)
    for n in range(4):
        grad_part(0, n)
    delta_items(1, mid, last)
    delta_end(1, last - 4, last - 1)
    for n in (0, 2):
        grad_part(1, n)
    delta_end(1, last - 1, last)
    for n in (1, 3):
        grad_part(1, n)

    for n in range(4):
        grad_copy(n).wait()
    others(sh, 0, hid_recv.at[nch]).wait_send()
    others(th, 1, hid_recv.at[nch]).wait_send()
    relay(sh, 0, core).wait_send()
    relay(th, 1, core).wait_send()
    for g in range(2):
        stats_copy(g).wait_send()
        for sem in (s_send, t_send, ag_send):
            pltpu.make_async_remote_copy(
                s_t.at[g], r_t.at[g], sem.at[g], t_recv.at[g, 0, 0], device_id={"dp": right}
            ).wait_send()


def body(teacher_hidden, teacher_weight, student_hidden, student_weight):
    nz, nv = lax.axis_size("dp"), lax.axis_size("vocab")
    rows, kt = teacher_hidden.shape
    ks, width = student_weight.shape
    nch = nv // 2
    cpq = nch // nz
    gr = cpq * rows
    cq = width // 4
    tc = min(256, cq)
    n_items = 4 * (nz // 2 - 1) + 2
    factor = float(width * nv // 4 / (rows * nv))
    dims = (nz, nv, cpq, gr, ks, kt, cq, tc, factor)
    dma = pltpu.SemaphoreType.DMA
    any_space = pl.BlockSpec(memory_space=pl.ANY)
    vmem = pl.BlockSpec(memory_space=pltpu.VMEM)
    kl, grad = pl.pallas_call(
        functools.partial(kernel, dims),
        out_shape=(
            jax.ShapeDtypeStruct((1, 128), F32),
            jax.ShapeDtypeStruct((ks, width), BF16),
        ),
        in_specs=[any_space] * 4,
        out_specs=(vmem, any_space),
        scratch_shapes=[
            pltpu.VMEM((2, nch, rows, kt), BF16),
            pltpu.VMEM((width // tc, kt, tc), BF16),
            pltpu.VMEM((2, nch, rows, ks), BF16),
            pltpu.VMEM((ks, width), BF16),
            pltpu.VMEM((nz, 2, 4, gr, cq), F32),
            pltpu.VMEM((nz, 2, 4, gr, cq), F32),
            *[pltpu.VMEM((2, 2, n_items, gr, cq), BF16)] * 4,
            pltpu.VMEM((2, 4, nz, gr, cq), BF16),
            pltpu.VMEM((4, ks, cq), F32),
            pltpu.VMEM((2, ks, nz * gr), BF16),
            pltpu.VMEM((2, nv, 16, 128), F32),
            pltpu.VMEM((4, ks, cq), BF16),
            dma((3 + width // tc,)),
            dma((2,)),
            dma((nch + 1,)),
            dma((2,)),
            dma((2,)),
            dma((4,)),
            dma((2,)),
            dma((2, 2, n_items)),
            dma((2,)),
            dma((2, 2, n_items)),
            dma((2,)),
            dma((2,)),
            dma((2,)),
            dma((2, 2, n_items)),
        ],
        compiler_params=pltpu.CompilerParams(
            collective_id=0, has_side_effects=True, vmem_limit_bytes=67_000_000
        ),
        name="distill",
    )(teacher_hidden, teacher_weight, student_hidden, student_weight)
    return kl.reshape(128)[: 2 * gr], grad


def solution(mesh):
    placed = (P("vocab", "dp"), P("dp", "vocab"), P("vocab", "dp"), P("dp", "vocab"))
    return jax.shard_map(
        body, mesh=mesh, in_specs=placed, out_specs=(P("dp"), P("dp", "vocab")), check_vma=False
    )
```

```python
import functools

import jax
import jax.numpy as jnp
from jax import lax
from jax.experimental import pallas as pl
from jax.experimental.pallas import tpu as pltpu
from jax.sharding import PartitionSpec as P

BF16 = jnp.bfloat16
F32 = jnp.float32
SCALE = 2.0**-7.75
LOG2E = 1.4426950408889634


def encode(x):
    t = jnp.abs(x) * SCALE + SCALE
    t = t * t
    t = t * t
    t = t * t
    t = t * t
    return jnp.where(x < 0, -t, t).astype(BF16)


def decode(word):
    y = word.astype(F32)
    t = jnp.exp2(jnp.log(jnp.abs(y)) * (LOG2E / 16) + 7.75) - 1.0
    return jnp.where(y < 0, -t, t)


def kernel(
    dims,
    th_hbm, tw_hbm, sh_hbm, sw_hbm,
    kl_out, grad_out,
    th, tw, sh, sw, pst, ptt, r_s, r_t, s_s, s_t, dl, acc, sht, stats,
    local_sem, hid_send, hid_recv, rel_send, rel_recv,
    s_send, s_recv, t_send, t_recv, st_send, st_recv, ag_send, ag_recv,
):
    nz, nv, cpq, gr, ks, kt, cq, tc, factor = dims
    nch = nv // 2
    n_items = 4 * (nz // 2 - 1) + 2
    p = lax.axis_index("dp")
    v = lax.axis_index("vocab")
    core = lax.rem(v, 2)
    chip = v // 2
    partner = v + 1 - 2 * core
    right, left = lax.rem(p + 1, nz), lax.rem(p + nz - 1, nz)
    ways = ((1, right), (-1, left))

    def at(offset):
        return lax.rem(p + offset + 2 * nz, nz)

    load_sw = pltpu.make_async_copy(sw_hbm, sw, local_sem.at[0])
    load_sh = pltpu.make_async_copy(sh_hbm, sh.at[core, chip], local_sem.at[1])
    load_th = pltpu.make_async_copy(th_hbm, th.at[core, chip], local_sem.at[2])
    load_sh.start()
    load_th.start()
    load_sw.start()
    n_tw = tw.shape[0]
    load_tw = [
        pltpu.make_async_copy(tw_hbm.at[:, j * tc : (j + 1) * tc], tw.at[j], local_sem.at[3 + j])
        for j in range(n_tw)
    ]
    for load in load_tw:
        load.start()

    barrier = pltpu.get_barrier_semaphore()

    def greet(j, _):
        pl.semaphore_signal(barrier, inc=1, device_id={"vocab": lax.rem(v + j, nv)})
        return 0

    lax.fori_loop(1, nv, greet, 0)
    for _, neighbour in ways:
        pl.semaphore_signal(barrier, inc=1, device_id={"dp": neighbour})
    pl.semaphore_wait(barrier, nv + 1)

    def spread(source, target, k, arrival):
        def one(j, _):
            peer = lax.rem(chip + j, nch)
            pltpu.make_async_remote_copy(
                source, target.at[core, chip], hid_send.at[k], arrival,
                device_id={"vocab": 2 * peer + core},
            ).start()
            return 0

        lax.fori_loop(1, nch, one, 0)

    def others(target, k, arrival):
        block = target.at[core, pl.ds(0, nch - 1)]
        return pltpu.make_async_remote_copy(
            block, block, hid_send.at[k], arrival, device_id={"vocab": partner}
        )

    def relay(target, k, slab):
        return pltpu.make_async_remote_copy(
            target.at[slab], target.at[slab], rel_send.at[k], rel_recv.at[k],
            device_id={"vocab": partner},
        )

    spread(sh_hbm, sh, 0, hid_recv.at[chip])
    spread(th_hbm, th, 1, hid_recv.at[nch])
    load_sh.wait()
    load_sw.wait()

    def student_block(q):
        for j in range(cpq):
            source = cpq * q + j

            @pl.when(source != chip)
            def _():
                block = sh.at[core, source]
                pltpu.make_async_remote_copy(
                    block, block, hid_send.at[0], hid_recv.at[source], device_id={"vocab": partner}
                ).wait_recv()

        rows = sh[core, pl.ds(cpq * q, cpq)].reshape(gr, ks)
        for n in range(4):
            part = jnp.dot(rows, sw[:, n * cq : (n + 1) * cq], preferred_element_type=F32)
            pst[q, core, n] = part

    def student_rest():
        rows = sh[1 - core].reshape(nz * gr, ks)
        for n in range(4):
            part = jnp.dot(rows, sw[:, n * cq : (n + 1) * cq], preferred_element_type=F32)
            pst[:, 1 - core, n] = part.reshape(nz, gr, cq)

    def teacher_part(g, j):
        rows = th[g].reshape(nz * gr, kt)
        part = jnp.dot(rows, tw[j], preferred_element_type=F32)
        per = cq // tc
        cols = pl.ds(pl.multiple_of(lax.rem(j, per) * tc, tc), tc)
        ptt[:, g, j // per, :, cols] = part.reshape(nz, gr, tc)

    student = (pst, s_s, r_s, s_send, s_recv)
    teacher = (ptt, s_t, r_t, t_send, t_recv)

    def ring_copy(which, g, d, i, neighbour):
        _, out, landed, sent, got = which
        return pltpu.make_async_remote_copy(
            out.at[g, d, i], landed.at[g, d, i], sent.at[g], got.at[g, d, i],
            device_id={"dp": neighbour},
        )

    def ring_items(which, g, lo, hi, more=None):
        part, out, landed, _, _ = which

        def one(i, _):
            k = nz // 2 - (i + 2) // 4
            for d, (sign, neighbour) in enumerate(ways):
                n = lax.rem(i + 2 * d, 4)
                x = part[at(sign * k), g, n]
                if lo >= 4:
                    ring_copy(which, g, d, i - 4, neighbour).wait_recv()
                    x = x + decode(landed[g, d, i - 4])
                out[g, d, i] = encode(x)
                ring_copy(which, g, d, i, neighbour).start()
            if more is not None:
                more(i)
            return 0

        lax.fori_loop(lo, hi, one, 0)

    def ring_end(which, g):
        part, _, landed, _, _ = which

        def one(j, _):
            i = n_items - 4 + j
            for d, (_, neighbour) in enumerate(ways):
                n = lax.rem(i + 2 * d, 4)
                ring_copy(which, g, d, i, neighbour).wait_recv()
                part[p, g, n] = part[p, g, n] + decode(landed[g, d, i])
            return 0

        lax.fori_loop(0, 4, one, 0)

    def stats_start(g):
        t_top = jnp.full((gr, 1), -jnp.inf, F32)
        s_top = t_top
        for n in range(4):
            t_top = jnp.maximum(t_top, jnp.max(ptt[p, g, n], axis=1, keepdims=True))
            s_top = jnp.maximum(s_top, jnp.max(pst[p, g, n], axis=1, keepdims=True))
        t_sum = jnp.zeros((gr, 1), F32)
        t_num, s_sum = t_sum, t_sum
        for n in range(4):
            t, s = ptt[p, g, n], pst[p, g, n]
            e = jnp.exp(t - t_top)
            t_sum = t_sum + jnp.sum(e, axis=1, keepdims=True)
            t_num = t_num + jnp.sum(e * (t - s), axis=1, keepdims=True)
            s_sum = s_sum + jnp.sum(jnp.exp(s - s_top), axis=1, keepdims=True)
        lane = lax.broadcasted_iota(jnp.int32, (gr, 128), 1)
        table = jnp.zeros((gr, 128), F32)
        for place, column in ((0, t_top), (1, t_top), (2, s_top), (8, t_sum), (9, t_num), (10, s_sum)):
            table = jnp.where(lane == place, column, table)
        sides = [table[r : r + gr // cpq] for r in range(0, gr, gr // cpq) for _ in range(2)]
        stats[g, v] = jnp.concatenate(sides * (64 // gr), axis=0).T[:16]

        def one(j, _):
            pltpu.make_async_remote_copy(
                stats.at[g, v], stats.at[g, v], st_send.at[g], st_recv.at[g],
                device_id={"vocab": lax.rem(v + j, nv)},
            ).start()
            return 0

        lax.fori_loop(1, nv, one, 0)

    def stats_copy(g):
        block = stats.at[g, pl.ds(0, nv - 1)]
        return pltpu.make_async_remote_copy(
            block, block, st_send.at[g], st_recv.at[g], device_id={"vocab": partner}
        )

    def deltas(g):
        stats_copy(g).wait_recv()
        tops = stats[g, :, 0:8]
        top = jnp.max(tops, axis=0)
        total = jnp.sum(jnp.exp(tops - top[None]) * stats[g, :, 8:16], axis=0)
        lse = top + jnp.log(total)
        kl = total[1:2] / total[0:1] - lse[0:1] + lse[2:3]
        if g == 0:
            kl_out[...] = kl
        else:
            lane = lax.broadcasted_iota(jnp.int32, (1, 128), 1)
            kl_out[...] = jnp.where(lane // (gr // cpq) % 2 == 1, kl, kl_out[...])
        turned = jnp.concatenate([lse] * 16, axis=0).T
        rows = gr // cpq
        turned = jnp.concatenate([turned[2 * r : 2 * r + rows] for r in range(0, gr, rows)], axis=0)
        t_lse, s_lse = turned[:, 0:1], turned[:, 2:3]
        for n in range(4):
            by_student = jnp.exp(pst[p, g, n] - s_lse)
            by_teacher = jnp.exp(ptt[p, g, n] - t_lse)
            dl[g, n, p] = (factor * (by_student - by_teacher)).astype(BF16)

    def delta_copy(g, d, i, sign, neighbour):
        n = lax.rem(i + 2 * d, 4)
        block = dl.at[g, n, at(-sign * (i // 4))]
        return pltpu.make_async_remote_copy(
            block, block, ag_send.at[g], ag_recv.at[g, d, i], device_id={"dp": neighbour}
        )

    def arrived(g, d, i, sign, neighbour):
        n = lax.rem(i + 2 * d, 4)
        block = dl.at[g, n, at(-sign * (i // 4 + 1))]
        return pltpu.make_async_remote_copy(
            block, block, ag_send.at[g], ag_recv.at[g, d, i], device_id={"dp": neighbour}
        )

    def delta_items(g, lo, hi):
        def one(i, _):
            for d, (sign, neighbour) in enumerate(ways):
                if lo >= 4:
                    arrived(g, d, i - 4, sign, neighbour).wait_recv()
                delta_copy(g, d, i, sign, neighbour).start()
            return 0

        lax.fori_loop(lo, hi, one, 0)

    def delta_end(g, lo, hi):
        def one(i, _):
            for d, (sign, neighbour) in enumerate(ways):
                arrived(g, d, i, sign, neighbour).wait_recv()
            return 0

        lax.fori_loop(lo, hi, one, 0)

    def grad_part(g, n):
        part = jnp.dot(sht[g], dl[g, n].reshape(nz * gr, cq), preferred_element_type=F32)
        if g == 0:
            acc[n] = part
        else:
            grad_out[:, n * cq : (n + 1) * cq] = (acc[n] + part).astype(BF16)

    last = n_items
    mid = max(4, last - 4)
    other = 1 - core
    student_block(at(nz // 2))
    ring_items(student, core, 0, 2)
    for k in range(nz // 2 - 1, 0, -1):
        student_block(at(k))
        student_block(at(-k))
        if k == nz // 2 - 1:
            ring_items(student, core, 2, 4)
    student_block(p)
    relay(sh, 0, core).start()
    ring_items(student, core, 4, mid)
    relay(sh, 0, other).wait_recv()
    student_rest()
    ring_items(student, other, 0, 4)
    ring_items(student, core, mid, last)
    load_th.wait()
    others(th, 1, hid_recv.at[nch]).wait_recv()
    relay(th, 1, core).start()
    ring_end(student, core)
    for load in load_tw:
        load.wait()

    def teacher_own(i):
        if n_items >= 14:
            teacher_part(core, 2 * (i - 4))
            teacher_part(core, 2 * (i - 4) + 1)

    def teacher_rest(i):
        if n_items >= 14:
            teacher_part(other, i - 8)

    def parts(slab, lo):
        def one(j, _):
            teacher_part(slab, j)
            return 0

        lax.fori_loop(lo, n_tw, one, 0)

    early = min(8, last)
    ring_items(student, other, 4, early, teacher_own)
    parts(core, 8 if n_items >= 14 else 0)
    relay(th, 1, other).wait_recv()
    ring_items(student, other, early, last, teacher_rest)
    parts(other, last - 8 if n_items >= 14 else 0)
    ring_items(teacher, 0, 0, 4)
    ring_end(student, other)
    for g in range(2):
        sht[g] = sh[g].reshape(nz * gr, ks).T
    ring_items(teacher, 0, 4, last)
    ring_items(teacher, 1, 0, 4)
    ring_end(teacher, 0)
    stats_start(0)
    ring_items(teacher, 1, 4, mid)
    deltas(0)
    delta_items(0, 0, 4)
    ring_items(teacher, 1, mid, last)
    delta_items(0, 4, early)
    ring_end(teacher, 1)
    stats_start(1)
    late = max(early, last - 2)
    delta_items(0, early, late)
    deltas(1)
    delta_items(1, 0, 4)
    delta_items(0, late, last)
    delta_items(1, 4, early)
    delta_end(0, last - 4, last)
    for n in range(4):
        grad_part(0, n)
    delta_items(1, early, last)
    delta_end(1, last - 4, last - 1)
    for n in (0, 2):
        grad_part(1, n)
    delta_end(1, last - 1, last)
    for n in (1, 3):
        grad_part(1, n)

    others(sh, 0, hid_recv.at[nch]).wait_send()
    others(th, 1, hid_recv.at[nch]).wait_send()
    relay(sh, 0, core).wait_send()
    relay(th, 1, core).wait_send()
    for g in range(2):
        stats_copy(g).wait_send()
        for sem in (s_send, t_send, ag_send):
            pltpu.make_async_remote_copy(
                s_t.at[g], r_t.at[g], sem.at[g], t_recv.at[g, 0, 0], device_id={"dp": right}
            ).wait_send()


def body(teacher_hidden, teacher_weight, student_hidden, student_weight):
    nz, nv = lax.axis_size("dp"), lax.axis_size("vocab")
    rows, kt = teacher_hidden.shape
    ks, width = student_weight.shape
    nch = nv // 2
    cpq = nch // nz
    gr = cpq * rows
    cq = width // 4
    tc = min(256, cq)
    n_items = 4 * (nz // 2 - 1) + 2
    factor = float(width * nv // 4 / (rows * nv))
    dims = (nz, nv, cpq, gr, ks, kt, cq, tc, factor)
    dma = pltpu.SemaphoreType.DMA
    any_space = pl.BlockSpec(memory_space=pl.ANY)
    vmem = pl.BlockSpec(memory_space=pltpu.VMEM)
    kl, grad = pl.pallas_call(
        functools.partial(kernel, dims),
        out_shape=(
            jax.ShapeDtypeStruct((1, 128), F32),
            pltpu.MemorySpace.VMEM((ks, width), BF16),
        ),
        in_specs=[any_space] * 4,
        out_specs=(vmem, vmem),
        scratch_shapes=[
            pltpu.VMEM((2, nch, rows, kt), BF16),
            pltpu.VMEM((width // tc, kt, tc), BF16),
            pltpu.VMEM((2, nch, rows, ks), BF16),
            pltpu.VMEM((ks, width), BF16),
            pltpu.VMEM((nz, 2, 4, gr, cq), F32),
            pltpu.VMEM((nz, 2, 4, gr, cq), F32),
            *[pltpu.VMEM((2, 2, n_items, gr, cq), BF16)] * 4,
            pltpu.VMEM((2, 4, nz, gr, cq), BF16),
            pltpu.VMEM((4, ks, cq), F32),
            pltpu.VMEM((2, ks, nz * gr), BF16),
            pltpu.VMEM((2, nv, 16, 128), F32),
            dma((3 + width // tc,)),
            dma((2,)),
            dma((nch + 1,)),
            dma((2,)),
            dma((2,)),
            dma((2,)),
            dma((2, 2, n_items)),
            dma((2,)),
            dma((2, 2, n_items)),
            dma((2,)),
            dma((2,)),
            dma((2,)),
            dma((2, 2, n_items)),
        ],
        compiler_params=pltpu.CompilerParams(
            collective_id=0, has_side_effects=True, vmem_limit_bytes=64_500_000
        ),
        name="distill",
    )(teacher_hidden, teacher_weight, student_hidden, student_weight)
    return kl.reshape(128)[: 2 * gr], grad


def solution(mesh):
    placed = (P("vocab", "dp"), P("dp", "vocab"), P("vocab", "dp"), P("dp", "vocab"))
    return jax.shard_map(
        body, mesh=mesh, in_specs=placed, out_specs=(P("dp"), P("dp", "vocab")), check_vma=False
    )
```

```python
import functools

import jax
import jax.numpy as jnp
from jax import lax
from jax.experimental import pallas as pl
from jax.experimental.pallas import tpu as pltpu
from jax.sharding import PartitionSpec as P

BF16 = jnp.bfloat16
F32 = jnp.float32
SCALE = 2.0**-7.75
LOG2E = 1.4426950408889634


def encode(x):
    t = jnp.abs(x) * SCALE + SCALE
    t = t * t
    t = t * t
    t = t * t
    t = t * t
    return jnp.where(x < 0, -t, t).astype(BF16)


def decode(word):
    y = word.astype(F32)
    t = jnp.exp2(jnp.log(jnp.abs(y)) * (LOG2E / 16) + 7.75) - 1.0
    return jnp.where(y < 0, -t, t)


def kernel(
    dims,
    th_hbm, tw_hbm, sh_hbm, sw_hbm,
    kl_out, grad_out,
    th, tw, sh, sw, pst, ptt, r_s, r_t, s_s, s_t, dl, acc, sht, stats,
    local_sem, hid_send, hid_recv, rel_send, rel_recv,
    s_send, s_recv, t_send, t_recv, st_send, st_recv, ag_send, ag_recv,
):
    nz, nv, cpq, gr, ks, kt, cq, tc, factor = dims
    nch = nv // 2
    n_items = 4 * (nz // 2 - 1) + 2
    p = lax.axis_index("dp")
    v = lax.axis_index("vocab")
    core = lax.rem(v, 2)
    chip = v // 2
    partner = v + 1 - 2 * core
    right, left = lax.rem(p + 1, nz), lax.rem(p + nz - 1, nz)
    ways = ((1, right), (-1, left))

    def at(offset):
        return lax.rem(p + offset + 2 * nz, nz)

    load_sw = pltpu.make_async_copy(sw_hbm, sw, local_sem.at[0])
    load_sh = pltpu.make_async_copy(sh_hbm, sh.at[core, chip], local_sem.at[1])
    load_th = pltpu.make_async_copy(th_hbm, th.at[core, chip], local_sem.at[2])
    load_sh.start()
    load_th.start()
    load_sw.start()
    n_tw = tw.shape[0]
    load_tw = [
        pltpu.make_async_copy(tw_hbm.at[:, j * tc : (j + 1) * tc], tw.at[j], local_sem.at[3 + j])
        for j in range(n_tw)
    ]
    for load in load_tw:
        load.start()

    barrier = pltpu.get_barrier_semaphore()

    def greet(j, _):
        pl.semaphore_signal(barrier, inc=1, device_id={"vocab": lax.rem(v + j, nv)})
        return 0

    lax.fori_loop(1, nv, greet, 0)
    for _, neighbour in ways:
        pl.semaphore_signal(barrier, inc=1, device_id={"dp": neighbour})
    pl.semaphore_wait(barrier, nv + 1)

    def spread(source, target, k, arrival):
        def one(j, _):
            peer = lax.rem(chip + j, nch)
            pltpu.make_async_remote_copy(
                source, target.at[core, chip], hid_send.at[k], arrival,
                device_id={"vocab": 2 * peer + core},
            ).start()
            return 0

        lax.fori_loop(1, nch, one, 0)

    def others(target, k, arrival):
        block = target.at[core, pl.ds(0, nch - 1)]
        return pltpu.make_async_remote_copy(
            block, block, hid_send.at[k], arrival, device_id={"vocab": partner}
        )

    def relay(target, k, slab):
        return pltpu.make_async_remote_copy(
            target.at[slab], target.at[slab], rel_send.at[k], rel_recv.at[k],
            device_id={"vocab": partner},
        )

    spread(sh_hbm, sh, 0, hid_recv.at[chip])
    spread(th_hbm, th, 1, hid_recv.at[nch])
    load_sh.wait()
    load_sw.wait()

    def student_block(q):
        for j in range(cpq):
            source = cpq * q + j

            @pl.when(source != chip)
            def _():
                block = sh.at[core, source]
                pltpu.make_async_remote_copy(
                    block, block, hid_send.at[0], hid_recv.at[source], device_id={"vocab": partner}
                ).wait_recv()

        rows = sh[core, pl.ds(cpq * q, cpq)].reshape(gr, ks)
        for n in range(4):
            part = jnp.dot(rows, sw[:, n * cq : (n + 1) * cq], preferred_element_type=F32)
            pst[q, core, n] = part

    def student_rest():
        rows = sh[1 - core].reshape(nz * gr, ks)
        for n in range(4):
            part = jnp.dot(rows, sw[:, n * cq : (n + 1) * cq], preferred_element_type=F32)
            pst[:, 1 - core, n] = part.reshape(nz, gr, cq)

    def teacher_part(g, j):
        rows = th[g].reshape(nz * gr, kt)
        part = jnp.dot(rows, tw[j], preferred_element_type=F32)
        per = cq // tc
        cols = pl.ds(pl.multiple_of(lax.rem(j, per) * tc, tc), tc)
        ptt[:, g, j // per, :, cols] = part.reshape(nz, gr, tc)

    student = (pst, s_s, r_s, s_send, s_recv)
    teacher = (ptt, s_t, r_t, t_send, t_recv)

    def ring_copy(which, g, d, i, neighbour):
        _, out, landed, sent, got = which
        return pltpu.make_async_remote_copy(
            out.at[g, d, i], landed.at[g, d, i], sent.at[g], got.at[g, d, i],
            device_id={"dp": neighbour},
        )

    def ring_items(which, g, lo, hi, more=None):
        part, out, landed, _, _ = which

        def one(i, _):
            k = nz // 2 - (i + 2) // 4
            for d, (sign, neighbour) in enumerate(ways):
                n = lax.rem(i + 2 * d, 4)
                x = part[at(sign * k), g, n]
                if lo >= 4:
                    ring_copy(which, g, d, i - 4, neighbour).wait_recv()
                    x = x + decode(landed[g, d, i - 4])
                out[g, d, i] = encode(x)
                ring_copy(which, g, d, i, neighbour).start()
            if more is not None:
                more(i)
            return 0

        lax.fori_loop(lo, hi, one, 0)

    def ring_end(which, g):
        part, _, landed, _, _ = which

        def one(j, _):
            i = n_items - 4 + j
            for d, (_, neighbour) in enumerate(ways):
                n = lax.rem(i + 2 * d, 4)
                ring_copy(which, g, d, i, neighbour).wait_recv()
                part[p, g, n] = part[p, g, n] + decode(landed[g, d, i])
            return 0

        lax.fori_loop(0, 4, one, 0)

    def stats_start(g):
        t_top = jnp.full((gr, 1), -jnp.inf, F32)
        s_top = t_top
        for n in range(4):
            t_top = jnp.maximum(t_top, jnp.max(ptt[p, g, n], axis=1, keepdims=True))
            s_top = jnp.maximum(s_top, jnp.max(pst[p, g, n], axis=1, keepdims=True))
        t_sum = jnp.zeros((gr, 1), F32)
        t_num, s_sum = t_sum, t_sum
        for n in range(4):
            t, s = ptt[p, g, n], pst[p, g, n]
            e = jnp.exp(t - t_top)
            t_sum = t_sum + jnp.sum(e, axis=1, keepdims=True)
            t_num = t_num + jnp.sum(e * (t - s), axis=1, keepdims=True)
            s_sum = s_sum + jnp.sum(jnp.exp(s - s_top), axis=1, keepdims=True)
        lane = lax.broadcasted_iota(jnp.int32, (gr, 128), 1)
        table = jnp.zeros((gr, 128), F32)
        for place, column in ((0, t_top), (1, t_top), (2, s_top), (8, t_sum), (9, t_num), (10, s_sum)):
            table = jnp.where(lane == place, column, table)
        sides = [table[r : r + gr // cpq] for r in range(0, gr, gr // cpq) for _ in range(2)]
        stats[g, v] = jnp.concatenate(sides * (64 // gr), axis=0).T[:16]

        def one(j, _):
            pltpu.make_async_remote_copy(
                stats.at[g, v], stats.at[g, v], st_send.at[g], st_recv.at[g],
                device_id={"vocab": lax.rem(v + j, nv)},
            ).start()
            return 0

        lax.fori_loop(1, nv, one, 0)

    def stats_copy(g):
        block = stats.at[g, pl.ds(0, nv - 1)]
        return pltpu.make_async_remote_copy(
            block, block, st_send.at[g], st_recv.at[g], device_id={"vocab": partner}
        )

    def deltas(g):
        stats_copy(g).wait_recv()
        tops = stats[g, :, 0:8]
        top = jnp.max(tops, axis=0)
        total = jnp.sum(jnp.exp(tops - top[None]) * stats[g, :, 8:16], axis=0)
        lse = top + jnp.log(total)
        kl = total[1:2] / total[0:1] - lse[0:1] + lse[2:3]
        if g == 0:
            kl_out[...] = kl
        else:
            lane = lax.broadcasted_iota(jnp.int32, (1, 128), 1)
            kl_out[...] = jnp.where(lane // (gr // cpq) % 2 == 1, kl, kl_out[...])
        turned = jnp.concatenate([lse] * 16, axis=0).T
        rows = gr // cpq
        turned = jnp.concatenate([turned[2 * r : 2 * r + rows] for r in range(0, gr, rows)], axis=0)
        t_lse, s_lse = turned[:, 0:1], turned[:, 2:3]
        for n in range(4):
            by_student = jnp.exp(pst[p, g, n] - s_lse)
            by_teacher = jnp.exp(ptt[p, g, n] - t_lse)
            dl[g, n, p] = (factor * (by_student - by_teacher)).astype(BF16)

    def delta_copy(g, d, i, sign, neighbour):
        n = lax.rem(i + 2 * d, 4)
        block = dl.at[g, n, at(-sign * (i // 4))]
        return pltpu.make_async_remote_copy(
            block, block, ag_send.at[g], ag_recv.at[g, d, i], device_id={"dp": neighbour}
        )

    def arrived(g, d, i, sign, neighbour):
        n = lax.rem(i + 2 * d, 4)
        block = dl.at[g, n, at(-sign * (i // 4 + 1))]
        return pltpu.make_async_remote_copy(
            block, block, ag_send.at[g], ag_recv.at[g, d, i], device_id={"dp": neighbour}
        )

    def delta_items(g, lo, hi):
        def one(i, _):
            for d, (sign, neighbour) in enumerate(ways):
                if lo >= 4:
                    arrived(g, d, i - 4, sign, neighbour).wait_recv()
                delta_copy(g, d, i, sign, neighbour).start()
            return 0

        lax.fori_loop(lo, hi, one, 0)

    def delta_end(g, lo, hi):
        def one(i, _):
            for d, (sign, neighbour) in enumerate(ways):
                arrived(g, d, i, sign, neighbour).wait_recv()
            return 0

        lax.fori_loop(lo, hi, one, 0)

    def grad_part(g, n):
        part = jnp.dot(sht[g], dl[g, n].reshape(nz * gr, cq), preferred_element_type=F32)
        if g == 0:
            acc[n] = part
        else:
            grad_out[:, n * cq : (n + 1) * cq] = (acc[n] + part).astype(BF16)

    last = n_items
    mid = max(4, last - 4)
    other = 1 - core
    student_block(at(nz // 2))
    ring_items(student, core, 0, 2)
    for k in range(nz // 2 - 1, 0, -1):
        student_block(at(k))
        student_block(at(-k))
        if k == nz // 2 - 1:
            ring_items(student, core, 2, 4)
    student_block(p)
    relay(sh, 0, core).start()
    ring_items(student, core, 4, mid)
    relay(sh, 0, other).wait_recv()
    student_rest()
    ring_items(student, other, 0, 4)
    ring_items(student, core, mid, last)
    ring_end(student, core)
    ring_items(student, other, 4, mid)
    load_th.wait()
    others(th, 1, hid_recv.at[nch]).wait_recv()
    relay(th, 1, core).start()
    late = max(mid, last - 2)
    ring_items(student, other, mid, late)
    for load in load_tw:
        load.wait()
    relay(th, 1, other).wait_recv()
    full = n_tw == 8 and n_items == 14

    def parts(g, lo):
        def one(j, _):
            teacher_part(g, j)
            return 0

        lax.fori_loop(lo, n_tw, one, 0)

    def first_parts(i):
        if full:
            teacher_part(0, 2 * (i - 12))
            teacher_part(0, 2 * (i - 12) + 1)

    def second_parts(i):
        if full:
            teacher_part(1, i - 4)

    ring_items(student, other, late, last, first_parts)
    parts(0, 4 if full else 0)
    ring_items(teacher, 0, 0, 4)
    ring_end(student, other)
    ring_items(teacher, 0, 4, min(12, last), second_parts)
    parts(1, 8 if full else 0)
    ring_items(teacher, 0, max(4, min(12, last)), last)
    ring_items(teacher, 1, 0, 4)
    ring_end(teacher, 0)
    stats_start(0)
    for g in range(2):
        sht[g] = sh[g].reshape(nz * gr, ks).T
    ring_items(teacher, 1, 4, mid)
    deltas(0)
    delta_items(0, 0, 4)
    ring_items(teacher, 1, mid, last)
    early = min(8, last)
    delta_items(0, 4, early)
    ring_end(teacher, 1)
    stats_start(1)
    late = max(early, last - 2)
    delta_items(0, early, late)
    deltas(1)
    delta_items(1, 0, 4)
    delta_items(0, late, last)
    delta_items(1, 4, early)
    delta_end(0, last - 4, last)
    for n in range(4):
        grad_part(0, n)
    delta_items(1, early, last)
    delta_end(1, last - 4, last - 1)
    for n in (0, 2):
        grad_part(1, n)
    delta_end(1, last - 1, last)
    for n in (1, 3):
        grad_part(1, n)

    others(sh, 0, hid_recv.at[nch]).wait_send()
    others(th, 1, hid_recv.at[nch]).wait_send()
    relay(sh, 0, core).wait_send()
    relay(th, 1, core).wait_send()
    for g in range(2):
        stats_copy(g).wait_send()
        for sem in (s_send, t_send, ag_send):
            pltpu.make_async_remote_copy(
                s_t.at[g], r_t.at[g], sem.at[g], t_recv.at[g, 0, 0], device_id={"dp": right}
            ).wait_send()


def body(teacher_hidden, teacher_weight, student_hidden, student_weight):
    nz, nv = lax.axis_size("dp"), lax.axis_size("vocab")
    rows, kt = teacher_hidden.shape
    ks, width = student_weight.shape
    nch = nv // 2
    cpq = nch // nz
    gr = cpq * rows
    cq = width // 4
    tc = min(256, cq)
    n_items = 4 * (nz // 2 - 1) + 2
    factor = float(width * nv // 4 / (rows * nv))
    dims = (nz, nv, cpq, gr, ks, kt, cq, tc, factor)
    dma = pltpu.SemaphoreType.DMA
    any_space = pl.BlockSpec(memory_space=pl.ANY)
    vmem = pl.BlockSpec(memory_space=pltpu.VMEM)
    kl, grad = pl.pallas_call(
        functools.partial(kernel, dims),
        out_shape=(
            jax.ShapeDtypeStruct((1, 128), F32),
            pltpu.MemorySpace.VMEM((ks, width), BF16),
        ),
        in_specs=[any_space] * 4,
        out_specs=(vmem, vmem),
        scratch_shapes=[
            pltpu.VMEM((2, nch, rows, kt), BF16),
            pltpu.VMEM((width // tc, kt, tc), BF16),
            pltpu.VMEM((2, nch, rows, ks), BF16),
            pltpu.VMEM((ks, width), BF16),
            pltpu.VMEM((nz, 2, 4, gr, cq), F32),
            pltpu.VMEM((nz, 2, 4, gr, cq), F32),
            *[pltpu.VMEM((2, 2, n_items, gr, cq), BF16)] * 4,
            pltpu.VMEM((2, 4, nz, gr, cq), BF16),
            pltpu.VMEM((4, ks, cq), F32),
            pltpu.VMEM((2, ks, nz * gr), BF16),
            pltpu.VMEM((2, nv, 16, 128), F32),
            dma((3 + width // tc,)),
            dma((2,)),
            dma((nch + 1,)),
            dma((2,)),
            dma((2,)),
            dma((2,)),
            dma((2, 2, n_items)),
            dma((2,)),
            dma((2, 2, n_items)),
            dma((2,)),
            dma((2,)),
            dma((2,)),
            dma((2, 2, n_items)),
        ],
        compiler_params=pltpu.CompilerParams(
            collective_id=0, has_side_effects=True, vmem_limit_bytes=64_500_000
        ),
        name="distill",
    )(teacher_hidden, teacher_weight, student_hidden, student_weight)
    return kl.reshape(128)[: 2 * gr], grad


def solution(mesh):
    placed = (P("vocab", "dp"), P("dp", "vocab"), P("vocab", "dp"), P("dp", "vocab"))
    return jax.shard_map(
        body, mesh=mesh, in_specs=placed, out_specs=(P("dp"), P("dp", "vocab")), check_vma=False
    )
```

```python
import functools

import jax
import jax.numpy as jnp
from jax import lax
from jax.experimental import pallas as pl
from jax.experimental.pallas import tpu as pltpu
from jax.sharding import PartitionSpec as P

BF16 = jnp.bfloat16
F32 = jnp.float32
SCALE = 2.0**-7.75
LOG2E = 1.4426950408889634


def encode(x):
    t = jnp.abs(x) * SCALE + SCALE
    t = t * t
    t = t * t
    t = t * t
    t = t * t
    return jnp.where(x < 0, -t, t).astype(BF16)


def decode(word):
    y = word.astype(F32)
    t = jnp.exp2(jnp.log(jnp.abs(y)) * (LOG2E / 16) + 7.75) - 1.0
    return jnp.where(y < 0, -t, t)


def kernel(
    dims,
    th_hbm, tw_hbm, sh_hbm, sw_hbm,
    kl_out, grad_out,
    th, tw, sh, sw, pst, ptt, r_s, r_t, s_s, s_t, dl, acc, sht, stats,
    local_sem, hid_send, hid_recv, rel_send, rel_recv,
    s_send, s_recv, t_send, t_recv, st_send, st_recv, ag_send, ag_recv,
):
    nz, nv, cpq, gr, ks, kt, cq, tc, factor = dims
    nch = nv // 2
    n_items = 4 * (nz // 2 - 1) + 2
    p = lax.axis_index("dp")
    v = lax.axis_index("vocab")
    core = lax.rem(v, 2)
    chip = v // 2
    partner = v + 1 - 2 * core
    right, left = lax.rem(p + 1, nz), lax.rem(p + nz - 1, nz)
    ways = ((1, right), (-1, left))

    def at(offset):
        return lax.rem(p + offset + 2 * nz, nz)

    load_sw = pltpu.make_async_copy(sw_hbm, sw, local_sem.at[0])
    load_sh = pltpu.make_async_copy(sh_hbm, sh.at[core, chip], local_sem.at[1])
    load_th = pltpu.make_async_copy(th_hbm, th.at[core, chip], local_sem.at[2])
    load_sh.start()
    load_th.start()
    load_sw.start()
    n_tw = tw.shape[0]
    load_tw = [
        pltpu.make_async_copy(tw_hbm.at[:, j * tc : (j + 1) * tc], tw.at[j], local_sem.at[3 + j])
        for j in range(n_tw)
    ]
    for load in load_tw:
        load.start()

    barrier = pltpu.get_barrier_semaphore()

    def greet(j, _):
        pl.semaphore_signal(barrier, inc=1, device_id={"vocab": lax.rem(v + j, nv)})
        return 0

    lax.fori_loop(1, nv, greet, 0)
    for _, neighbour in ways:
        pl.semaphore_signal(barrier, inc=1, device_id={"dp": neighbour})
    pl.semaphore_wait(barrier, nv + 1)

    def spread(source, target, k, arrival):
        def one(j, _):
            peer = lax.rem(chip + j, nch)
            pltpu.make_async_remote_copy(
                source, target.at[core, chip], hid_send.at[k], arrival,
                device_id={"vocab": 2 * peer + core},
            ).start()
            return 0

        lax.fori_loop(1, nch, one, 0)

    def others(target, k, arrival):
        block = target.at[core, pl.ds(0, nch - 1)]
        return pltpu.make_async_remote_copy(
            block, block, hid_send.at[k], arrival, device_id={"vocab": partner}
        )

    def relay(target, k, slab):
        return pltpu.make_async_remote_copy(
            target.at[slab], target.at[slab], rel_send.at[k], rel_recv.at[k],
            device_id={"vocab": partner},
        )

    spread(sh_hbm, sh, 0, hid_recv.at[chip])
    side = 4
    turns = nch == side * side

    def chip_at(dx, dy):
        return lax.rem(chip // side + dy + side, side) * side + lax.rem(chip + dx + side, side)

    def block_copy(source, block, to):
        return pltpu.make_async_remote_copy(
            source, th.at[core, block], hid_send.at[1], hid_recv.at[nch + block],
            device_id={"vocab": 2 * to + core},
        )

    def teacher_direct():
        spread(th_hbm, th, 1, hid_recv.at[nch + chip])

    def teacher_near():
        for dx, dy in ((3, 0), (0, 3), (3, 1), (1, 3), (3, 3), (1, 0), (0, 1), (1, 1)):
            block_copy(th_hbm, chip, chip_at(dx, dy)).start()

    if turns:
        pl.when(core == 0)(teacher_direct)
        pl.when(core == 1)(teacher_near)
    else:
        teacher_direct()

    def teacher_from(block):
        block_copy(th.at[core, block], block, lax.rem(chip + 1, nch)).wait_recv()

    def teacher_forward(a, b, steps):
        block = chip_at(-a, -b)
        teacher_from(block)

        @pl.when(core == 1)
        def _():
            for dx, dy in steps:
                block_copy(th.at[core, block], block, chip_at(dx, dy)).start()

    def forwards(group):
        if turns:
            for item in group:
                teacher_forward(*item)

    west, north = (-1, 0), (0, -1)
    first_forwards = ((3, 0, (west,)), (0, 3, (north,)))
    second_forwards = ((3, 1, (west,)), (1, 3, (north,)), (3, 3, (west, north)))
    third_forwards = ((2, 3, (north,)),)

    def teacher_others():
        if turns:
            for a, b in ((0, 1), (1, 0), (1, 1), (0, 2), (2, 0), (1, 2), (2, 1), (3, 2), (2, 2)):
                teacher_from(chip_at(-a, -b))
        else:

            def one(j, _):
                teacher_from(lax.rem(chip + j, nch))
                return 0

            lax.fori_loop(1, nch, one, 0)

    load_sh.wait()
    load_sw.wait()

    def student_block(q):
        for j in range(cpq):
            source = cpq * q + j

            @pl.when(source != chip)
            def _():
                block = sh.at[core, source]
                pltpu.make_async_remote_copy(
                    block, block, hid_send.at[0], hid_recv.at[source], device_id={"vocab": partner}
                ).wait_recv()

        rows = sh[core, pl.ds(cpq * q, cpq)].reshape(gr, ks)
        for n in range(4):
            part = jnp.dot(rows, sw[:, n * cq : (n + 1) * cq], preferred_element_type=F32)
            pst[q, core, n] = part

    def student_rest():
        rows = sh[1 - core].reshape(nz * gr, ks)
        for n in range(4):
            part = jnp.dot(rows, sw[:, n * cq : (n + 1) * cq], preferred_element_type=F32)
            pst[:, 1 - core, n] = part.reshape(nz, gr, cq)

    def teacher_part(g, j):
        rows = th[g].reshape(nz * gr, kt)
        part = jnp.dot(rows, tw[j], preferred_element_type=F32)
        per = cq // tc
        cols = pl.ds(pl.multiple_of(lax.rem(j, per) * tc, tc), tc)
        ptt[:, g, j // per, :, cols] = part.reshape(nz, gr, tc)

    student = (pst, s_s, r_s, s_send, s_recv)
    teacher = (ptt, s_t, r_t, t_send, t_recv)

    def ring_copy(which, g, d, i, neighbour):
        _, out, landed, sent, got = which
        return pltpu.make_async_remote_copy(
            out.at[g, d, i], landed.at[g, d, i], sent.at[g], got.at[g, d, i],
            device_id={"dp": neighbour},
        )

    def ring_items(which, g, lo, hi, more=None):
        part, out, landed, _, _ = which

        def one(i, _):
            k = nz // 2 - (i + 2) // 4
            for d, (sign, neighbour) in enumerate(ways):
                n = lax.rem(i + 2 * d, 4)
                x = part[at(sign * k), g, n]
                if lo >= 4:
                    ring_copy(which, g, d, i - 4, neighbour).wait_recv()
                    x = x + decode(landed[g, d, i - 4])
                out[g, d, i] = encode(x)
                ring_copy(which, g, d, i, neighbour).start()
            if more is not None:
                more(i)
            return 0

        lax.fori_loop(lo, hi, one, 0)

    def ring_end(which, g):
        part, _, landed, _, _ = which

        def one(j, _):
            i = n_items - 4 + j
            for d, (_, neighbour) in enumerate(ways):
                n = lax.rem(i + 2 * d, 4)
                ring_copy(which, g, d, i, neighbour).wait_recv()
                part[p, g, n] = part[p, g, n] + decode(landed[g, d, i])
            return 0

        lax.fori_loop(0, 4, one, 0)

    def stats_start(g):
        t_top = jnp.full((gr, 1), -jnp.inf, F32)
        s_top = t_top
        for n in range(4):
            t_top = jnp.maximum(t_top, jnp.max(ptt[p, g, n], axis=1, keepdims=True))
            s_top = jnp.maximum(s_top, jnp.max(pst[p, g, n], axis=1, keepdims=True))
        t_sum = jnp.zeros((gr, 1), F32)
        t_num, s_sum = t_sum, t_sum
        for n in range(4):
            t, s = ptt[p, g, n], pst[p, g, n]
            e = jnp.exp(t - t_top)
            t_sum = t_sum + jnp.sum(e, axis=1, keepdims=True)
            t_num = t_num + jnp.sum(e * (t - s), axis=1, keepdims=True)
            s_sum = s_sum + jnp.sum(jnp.exp(s - s_top), axis=1, keepdims=True)
        lane = lax.broadcasted_iota(jnp.int32, (gr, 128), 1)
        table = jnp.zeros((gr, 128), F32)
        for place, column in ((0, t_top), (1, t_top), (2, s_top), (8, t_sum), (9, t_num), (10, s_sum)):
            table = jnp.where(lane == place, column, table)
        sides = [table[r : r + gr // cpq] for r in range(0, gr, gr // cpq) for _ in range(2)]
        stats[g, v] = jnp.concatenate(sides * (64 // gr), axis=0).T[:16]

        def one(j, _):
            pltpu.make_async_remote_copy(
                stats.at[g, v], stats.at[g, v], st_send.at[g], st_recv.at[g],
                device_id={"vocab": lax.rem(v + j, nv)},
            ).start()
            return 0

        lax.fori_loop(1, nv, one, 0)

    def stats_copy(g):
        block = stats.at[g, pl.ds(0, nv - 1)]
        return pltpu.make_async_remote_copy(
            block, block, st_send.at[g], st_recv.at[g], device_id={"vocab": partner}
        )

    def deltas(g):
        stats_copy(g).wait_recv()
        tops = stats[g, :, 0:8]
        top = jnp.max(tops, axis=0)
        total = jnp.sum(jnp.exp(tops - top[None]) * stats[g, :, 8:16], axis=0)
        lse = top + jnp.log(total)
        kl = total[1:2] / total[0:1] - lse[0:1] + lse[2:3]
        if g == 0:
            kl_out[...] = kl
        else:
            lane = lax.broadcasted_iota(jnp.int32, (1, 128), 1)
            kl_out[...] = jnp.where(lane // (gr // cpq) % 2 == 1, kl, kl_out[...])
        turned = jnp.concatenate([lse] * 16, axis=0).T
        rows = gr // cpq
        turned = jnp.concatenate([turned[2 * r : 2 * r + rows] for r in range(0, gr, rows)], axis=0)
        t_lse, s_lse = turned[:, 0:1], turned[:, 2:3]
        for n in range(4):
            by_student = jnp.exp(pst[p, g, n] - s_lse)
            by_teacher = jnp.exp(ptt[p, g, n] - t_lse)
            dl[g, n, p] = (factor * (by_student - by_teacher)).astype(BF16)

    def delta_copy(g, d, i, sign, neighbour):
        n = lax.rem(i + 2 * d, 4)
        block = dl.at[g, n, at(-sign * (i // 4))]
        return pltpu.make_async_remote_copy(
            block, block, ag_send.at[g], ag_recv.at[g, d, i], device_id={"dp": neighbour}
        )

    def arrived(g, d, i, sign, neighbour):
        n = lax.rem(i + 2 * d, 4)
        block = dl.at[g, n, at(-sign * (i // 4 + 1))]
        return pltpu.make_async_remote_copy(
            block, block, ag_send.at[g], ag_recv.at[g, d, i], device_id={"dp": neighbour}
        )

    def delta_items(g, lo, hi):
        def one(i, _):
            for d, (sign, neighbour) in enumerate(ways):
                if lo >= 4:
                    arrived(g, d, i - 4, sign, neighbour).wait_recv()
                delta_copy(g, d, i, sign, neighbour).start()
            return 0

        lax.fori_loop(lo, hi, one, 0)

    def delta_end(g, lo, hi):
        def one(i, _):
            for d, (sign, neighbour) in enumerate(ways):
                arrived(g, d, i, sign, neighbour).wait_recv()
            return 0

        lax.fori_loop(lo, hi, one, 0)

    def grad_part(g, n):
        part = jnp.dot(sht[g], dl[g, n].reshape(nz * gr, cq), preferred_element_type=F32)
        if g == 0:
            acc[n] = part
        else:
            grad_out[:, n * cq : (n + 1) * cq] = (acc[n] + part).astype(BF16)

    last = n_items
    mid = max(4, last - 4)
    other = 1 - core
    student_block(at(nz // 2))
    ring_items(student, core, 0, 2)
    for k in range(nz // 2 - 1, 0, -1):
        student_block(at(k))
        student_block(at(-k))
        if k == nz // 2 - 1:
            ring_items(student, core, 2, 4)
    student_block(p)
    relay(sh, 0, core).start()
    ring_items(student, core, 4, mid)
    forwards(first_forwards)
    relay(sh, 0, other).wait_recv()
    student_rest()
    ring_items(student, other, 0, 4)
    forwards(second_forwards)
    ring_items(student, core, mid, last)
    forwards(third_forwards)
    load_th.wait()
    teacher_others()
    relay(th, 1, core).start()
    ring_end(student, core)
    for load in load_tw:
        load.wait()

    def teacher_own(i):
        if n_items >= 14:
            teacher_part(core, 2 * (i - 4))
            teacher_part(core, 2 * (i - 4) + 1)

    def teacher_rest(i):
        if n_items >= 14:
            teacher_part(other, i - 8)

    def parts(slab, lo):
        def one(j, _):
            teacher_part(slab, j)
            return 0

        lax.fori_loop(lo, n_tw, one, 0)

    early = min(8, last)
    ring_items(student, other, 4, early, teacher_own)
    parts(core, 8 if n_items >= 14 else 0)
    relay(th, 1, other).wait_recv()
    ring_items(student, other, early, last, teacher_rest)
    parts(other, last - 8 if n_items >= 14 else 0)
    ring_items(teacher, 0, 0, 4)
    ring_end(student, other)
    for g in range(2):
        sht[g] = sh[g].reshape(nz * gr, ks).T
    ring_items(teacher, 0, 4, last)
    ring_items(teacher, 1, 0, 4)
    ring_end(teacher, 0)
    stats_start(0)
    ring_items(teacher, 1, 4, mid)
    deltas(0)
    delta_items(0, 0, 4)
    ring_items(teacher, 1, mid, last)
    delta_items(0, 4, early)
    ring_end(teacher, 1)
    stats_start(1)
    late = max(early, last - 2)
    delta_items(0, early, late)
    deltas(1)
    delta_items(1, 0, 4)
    delta_items(0, late, last)
    delta_items(1, 4, early)
    delta_end(0, last - 4, last)
    for n in range(4):
        grad_part(0, n)
    delta_items(1, early, last)
    delta_end(1, last - 4, last - 1)
    for n in (0, 2):
        grad_part(1, n)
    delta_end(1, last - 1, last)
    for n in (1, 3):
        grad_part(1, n)

    others(sh, 0, hid_recv.at[nch]).wait_send()
    others(th, 1, hid_recv.at[nch]).wait_send()
    relay(sh, 0, core).wait_send()
    relay(th, 1, core).wait_send()
    for g in range(2):
        stats_copy(g).wait_send()
        for sem in (s_send, t_send, ag_send):
            pltpu.make_async_remote_copy(
                s_t.at[g], r_t.at[g], sem.at[g], t_recv.at[g, 0, 0], device_id={"dp": right}
            ).wait_send()


def body(teacher_hidden, teacher_weight, student_hidden, student_weight):
    nz, nv = lax.axis_size("dp"), lax.axis_size("vocab")
    rows, kt = teacher_hidden.shape
    ks, width = student_weight.shape
    nch = nv // 2
    cpq = nch // nz
    gr = cpq * rows
    cq = width // 4
    tc = min(256, cq)
    n_items = 4 * (nz // 2 - 1) + 2
    factor = float(width * nv // 4 / (rows * nv))
    dims = (nz, nv, cpq, gr, ks, kt, cq, tc, factor)
    dma = pltpu.SemaphoreType.DMA
    any_space = pl.BlockSpec(memory_space=pl.ANY)
    vmem = pl.BlockSpec(memory_space=pltpu.VMEM)
    kl, grad = pl.pallas_call(
        functools.partial(kernel, dims),
        out_shape=(
            jax.ShapeDtypeStruct((1, 128), F32),
            pltpu.MemorySpace.VMEM((ks, width), BF16),
        ),
        in_specs=[any_space] * 4,
        out_specs=(vmem, vmem),
        scratch_shapes=[
            pltpu.VMEM((2, nch, rows, kt), BF16),
            pltpu.VMEM((width // tc, kt, tc), BF16),
            pltpu.VMEM((2, nch, rows, ks), BF16),
            pltpu.VMEM((ks, width), BF16),
            pltpu.VMEM((nz, 2, 4, gr, cq), F32),
            pltpu.VMEM((nz, 2, 4, gr, cq), F32),
            *[pltpu.VMEM((2, 2, n_items, gr, cq), BF16)] * 4,
            pltpu.VMEM((2, 4, nz, gr, cq), BF16),
            pltpu.VMEM((4, ks, cq), F32),
            pltpu.VMEM((2, ks, nz * gr), BF16),
            pltpu.VMEM((2, nv, 16, 128), F32),
            dma((3 + width // tc,)),
            dma((2,)),
            dma((2 * nch,)),
            dma((2,)),
            dma((2,)),
            dma((2,)),
            dma((2, 2, n_items)),
            dma((2,)),
            dma((2, 2, n_items)),
            dma((2,)),
            dma((2,)),
            dma((2,)),
            dma((2, 2, n_items)),
        ],
        compiler_params=pltpu.CompilerParams(
            collective_id=0, has_side_effects=True, vmem_limit_bytes=64_500_000
        ),
        name="distill",
    )(teacher_hidden, teacher_weight, student_hidden, student_weight)
    return kl.reshape(128)[: 2 * gr], grad


def solution(mesh):
    placed = (P("vocab", "dp"), P("dp", "vocab"), P("vocab", "dp"), P("dp", "vocab"))
    return jax.shard_map(
        body, mesh=mesh, in_specs=placed, out_specs=(P("dp"), P("dp", "vocab")), check_vma=False
    )
```
